32 devices in a mesh: dp: 16 (over z, y, x), mp: 2 (over core).
Axes of the slice: x: 2, y: 2, z: 4, core: 2. Of those that a mesh axis runs over, the one named last changes fastest.
Arguments:
- head_out: bfloat16 [3, 2048, 4096], P(None, 'dp', 'mp'), may hold values from -6 to 6
- residual: bfloat16 [3, 2048, 4096], P(None, 'dp', 'mp'), may hold values from -6 to 6
- out_weight: bfloat16 [4096, 4096], P('dp', 'mp'), may hold values from -0.09375 to 0.09375
- strategy_table: bfloat16 [64, 4096], P(None, 'mp'), may hold values from -3 to 3
- meta_graph: int32 [64, 64], replicated, may hold values from 0 to 3, as said below
- strategy_ids: int32 [3, 2048], P(None, 'dp'), may hold values from 0 to 63
- cotangent: bfloat16 [3, 2048, 4096], P(None, 'dp', 'mp'), may hold values from -6 to 6
Outputs:
- layer_out: bfloat16 [3, 2048, 4096], P(None, 'dp', 'mp')
- head_grad: bfloat16 [3, 2048, 4096], P(None, 'dp', 'mp')
- weight_grad: float32 [4096, 4096], P('dp', 'mp')
- table_grad: float32 [64, 4096], P(None, 'mp')
The draws below stay inside these ranges and needn't reach their ends.
Inputs may be any that keep to these rules, and one draw needn't show every extreme that they name: `meta_graph`: entries are zero on and above the diagonal; the last strategy meets the first with weight 3.
All inputs are finite; a program needn't handle non-finite values.
Results may differ from the reference program's by a relative error of at most 0.009.
Values may be sent and summed in bfloat16 or wider, within the bound.
A program may use at most 192 MiB of HBM per device.

```python
import jax
import jax.numpy as jnp
from jax import lax

D = 4096
HEADS = 32
HD = 128
STRATS = 64
MB = 3
TOKENS = 2048
N_MP = 2


def draw_meta_graph(key, part):
    values = jax.random.randint(key, (STRATS, STRATS), 0, 4, dtype=jnp.int32)
    rows = lax.broadcasted_iota(jnp.int32, (STRATS, STRATS), 0)
    cols = lax.broadcasted_iota(jnp.int32, (STRATS, STRATS), 1)
    values = jnp.where(cols < rows, values, 0)
    values = jnp.where((rows == STRATS - 1) & (cols == 0), 3, values)
    return values.astype(jnp.int32)


def set_ends(result, stream_key, low, top_value):
    extent = result.shape
    spot = [jax.random.randint(jax.random.fold_in(stream_key, axis), (), 0, extent[axis]) for axis in range(len(extent))]
    result = result.at[tuple(spot)].set(low)
    longest = extent.index(max(extent))
    spot[longest] = (spot[longest] + 1) % extent[longest]
    return result.at[tuple(spot)].set(top_value)


def with_spikes(array, rng, source, target, shards_of, factor):
    def block_of(position):
        return (jnp.arange(array.shape[position]) // (array.shape[position] // shards_of)).reshape((-1,) + (1,) * (array.ndim - 1 - position))

    one_side = jax.random.permutation(rng, shards_of)[block_of(target)]
    other_side = (block_of(target) + shards_of // 2) % shards_of
    return jnp.where((block_of(source) == one_side) | (block_of(source) == other_side), factor * array, array)


def levels(stream_key, extent, pieces, low, top_value):
    level = 1.0
    for dim, parts in pieces:
        draws = jax.random.uniform(jax.random.fold_in(jax.random.fold_in(stream_key, 6), dim), (parts,), jnp.float32, low / len(pieces), top_value / len(pieces))
        level = level * jnp.repeat(jnp.exp(draws), extent[dim] // parts).reshape((-1,) + (1,) * (len(extent) - 1 - dim))
    return level


def centred(stream_key, extent, spread, limit, pieces=(), kind=jnp.bfloat16):
    array = spread * jax.random.normal(stream_key, extent, jnp.float32)
    if pieces:
        array = array * levels(stream_key, extent, pieces, -0.22, 0.18)
    return jnp.clip(array, -limit, limit).astype(kind)


def gaussian_with(key, dims, deviation, reach, cuts, heavy, kind=jnp.bfloat16):
    array = deviation * jax.random.normal(key, dims, jnp.float32)
    if cuts:
        array = array * levels(key, dims, cuts, -0.22, 0.18)
    return jnp.clip(with_spikes(array, jax.random.fold_in(key, 3), *heavy), -reach, reach).astype(kind)


def setup_inputs(seed: int = 0) -> dict:
    streams_of = jax.random.split(jax.random.key(seed), 8)
    head_out = centred(streams_of[0], (MB, TOKENS, HEADS * HD), 1.0, 6.0, ((1, 16), (2, 2)))
    residual = centred(streams_of[1], (MB, TOKENS, D), 1.0, 6.0, ((1, 16), (2, 2)))
    out_weight = centred(streams_of[2], (D, HEADS * HD), (HEADS * HD) ** -0.5, 0.09375, ((0, 16), (1, 2)))
    strategy_table = centred(streams_of[3], (STRATS, D), 0.5, 3.0, ((1, 2),))
    meta_graph = draw_meta_graph(jax.random.fold_in(streams_of[7], 71), 0)
    strategy_ids = set_ends(jax.random.randint(streams_of[5], (MB, TOKENS), 0, STRATS), jax.random.fold_in(streams_of[5], 1), 0, STRATS - 1).astype(jnp.int32)
    cotangent = gaussian_with(streams_of[6], (MB, TOKENS, D), 1.0, 6.0, ((1, 16), (2, 2)), (1, 2, 16, 2.0))
    return dict(head_out=head_out, residual=residual, out_weight=out_weight, strategy_table=strategy_table, meta_graph=meta_graph, strategy_ids=strategy_ids, cotangent=cotangent)


def mixture(meta_graph):
    counts = meta_graph.astype(jnp.float32)
    totals = jnp.maximum(lax.optimization_barrier(jnp.sum(counts, axis=1, keepdims=True)), 1.0)
    return jnp.eye(STRATS, dtype=jnp.float32) + counts / totals

def reference(head_out, residual, out_weight, strategy_table, meta_graph, strategy_ids, cotangent):
    highest = lax.Precision.HIGHEST
    mixing = mixture(meta_graph)
    table = jnp.dot(mixing, strategy_table.astype(jnp.float32), precision=highest)
    group_cols = HEADS * HD // N_MP
    grad_scale = 1.0 / jnp.sqrt(jnp.float32(MB * TOKENS))
    weight_sum = jnp.zeros((D, HEADS * HD), jnp.float32)
    table_sum = jnp.zeros((STRATS, D), jnp.float32)
    outputs = []
    head_grads = []
    for batch in range(MB):
        current = head_out[batch]
        projected = jnp.zeros((TOKENS, D), jnp.float32)
        for group in range(N_MP):
            lower = group * group_cols
            partial_sum = lax.dot_general(current[:, lower:lower + group_cols], out_weight[:, lower:lower + group_cols], (((1,), (1,)), ((), ())), preferred_element_type=jnp.float32)
            rounded = lax.optimization_barrier(partial_sum.astype(jnp.bfloat16))
            projected = projected + rounded.astype(jnp.float32)
        one_hot = (strategy_ids[batch][:, None] == jnp.arange(STRATS, dtype=jnp.int32)[None, :]).astype(jnp.float32)
        gating = 1.0 + jnp.dot(one_hot, table, precision=highest)
        outputs.append((residual[batch].astype(jnp.float32) + projected * gating).astype(jnp.bfloat16))
        grad_rows = (cotangent[batch].astype(jnp.float32) * gating).astype(jnp.bfloat16)
        head_grads.append(jnp.dot(grad_rows, out_weight, preferred_element_type=jnp.float32).astype(jnp.bfloat16))
        weight_sum = weight_sum + lax.dot_general(grad_rows, current, (((0,), (0,)), ((), ())), preferred_element_type=jnp.float32)
        cond_grad = cotangent[batch].astype(jnp.float32) * projected
        table_sum = table_sum + lax.dot_general(one_hot, cond_grad, (((0,), (0,)), ((), ())), precision=highest, preferred_element_type=jnp.float32)
    weight_grad = weight_sum * grad_scale
    table_grad = jnp.dot(mixing.T, table_sum, precision=highest) * grad_scale
    return (jnp.stack(outputs), jnp.stack(head_grads), weight_grad, table_grad)
```

```python
import math

import jax
import jax.numpy as jnp
from jax import lax
from jax.sharding import PartitionSpec as P


def inner_size(count):
    return 1 << ((count.bit_length() - 1) // 2)


def mixture(meta_graph):
    counts = meta_graph.astype(jnp.float32)
    totals = jnp.maximum(jnp.sum(counts, axis=1, keepdims=True), 1.0)
    return jnp.eye(meta_graph.shape[0], dtype=jnp.float32) + counts / totals


def swap(value, axis, offset):
    count = lax.axis_size(axis)
    return lax.ppermute(value, axis, [(i, i ^ offset) for i in range(count)])


def by_index(relative, index):
    stacked = jnp.stack(relative)
    return [
        lax.dynamic_index_in_dim(stacked, index ^ place, 0, keepdims=False)
        for place in range(len(relative))
    ]


def bit_orders(inner):
    bits = [1 << b for b in range(inner.bit_length() - 1)]
    return bits, bits[::-1]


def gather_rows(rows, inner):
    half = rows.shape[0] // 2
    parts = []
    for side, order in enumerate(bit_orders(inner)):
        have = {0: rows[side * half:(side + 1) * half]}
        for bit in order:
            keys = sorted(have)
            got = swap(jnp.concatenate([have[k] for k in keys]), "dp", bit)
            for place, key in enumerate(keys):
                have[key ^ bit] = got[place * half:(place + 1) * half]
        parts.append(have)
    return jnp.concatenate([parts[s][k] for k in range(inner) for s in range(2)])


def scatter_rows(partial, inner):
    rows = partial.shape[0] // inner
    half = rows // 2
    sums = []
    for side, order in enumerate(bit_orders(inner)):
        have = {
            k: partial[k * rows + side * half:k * rows + (side + 1) * half] for k in range(inner)
        }
        for bit in order[::-1]:
            going = [k for k in sorted(have) if k & bit]
            got = swap(
                jnp.concatenate([have[k].astype(jnp.bfloat16) for k in going]), "dp", bit
            )
            for place, key in enumerate(going):
                kept = have[key ^ bit].astype(jnp.float32)
                have[key ^ bit] = kept + got[place * half:(place + 1) * half].astype(jnp.float32)
                del have[key]
        sums.append(have[0])
    return jnp.concatenate(sums)


def line_pairs(inner, outer, step, first, last):
    return [
        (o * inner + i, (o + step) * inner + i) for o in range(first, last) for i in range(inner)
    ]


def gather_line(block, inner, outer, place):
    up, down, from_below, from_above = block, block, [], []
    for step in range(1, outer):
        up = lax.ppermute(up, "dp", line_pairs(inner, outer, 1, step - 1, outer - 1))
        down = lax.ppermute(down, "dp", line_pairs(inner, outer, -1, 1, outer - step + 1))
        from_below.append(up)
        from_above.append(down)
    size = block.shape[0]
    whole = jnp.zeros((outer * size,) + block.shape[1:], block.dtype)
    whole = lax.dynamic_update_slice_in_dim(whole, block, place * size, 0)
    for step in range(1, outer):
        piece = jnp.where(place >= step, from_below[step - 1], from_above[outer - step - 1])
        spot = lax.rem(place - step + outer, outer) * size
        whole = lax.dynamic_update_slice_in_dim(whole, piece, spot, 0)
    return whole


def scatter_line(partial, inner, outer, place):
    size = partial.shape[0] // outer

    def own(which):
        spot = jnp.clip(which, 0, outer - 1) * size
        return lax.dynamic_slice_in_dim(partial, spot, size, 0)

    up = own(place + outer - 1)
    down = own(place - outer + 1)
    for step in range(1, outer):
        up = lax.ppermute(up, "dp", line_pairs(inner, outer, 1, 0, step))
        down = lax.ppermute(down, "dp", line_pairs(inner, outer, -1, outer - step, outer))
        if step + 1 < outer:
            mine = own(place + outer - step - 1).astype(jnp.float32)
            up = (up.astype(jnp.float32) + mine).astype(jnp.bfloat16)
            mine = own(place - outer + step + 1).astype(jnp.float32)
            down = (down.astype(jnp.float32) + mine).astype(jnp.bfloat16)
    return own(place).astype(jnp.float32) + (up.astype(jnp.float32) + down.astype(jnp.float32))


def on_device(head_out, residual, out_weight, strategy_table, meta_graph, strategy_ids, cotangent):
    highest = lax.Precision.HIGHEST
    devices, groups = lax.axis_size("dp"), lax.axis_size("mp")
    inner = inner_size(devices)
    outer = devices // inner
    spans = outer // groups
    me, group = lax.axis_index("dp"), lax.axis_index("mp")
    near, far = lax.rem(me, inner), lax.div(me, inner)
    batches, local_rows, head_cols = head_out.shape
    rows = batches * local_rows
    strategies = meta_graph.shape[0]
    block = out_weight.shape[0]
    width = spans * block
    grad_scale = 1.0 / math.sqrt(batches * local_rows * devices)

    def features_of(array, which):
        return jnp.concatenate(
            [
                lax.dynamic_slice_in_dim(array, (s * inner + which) * block, block, 1)
                for s in range(spans)
            ],
            axis=1,
        )

    def over_groups(value):
        return by_index([value] + [swap(value, "mp", k) for k in range(1, groups)], group)

    cot_local = cotangent.reshape(rows, -1)
    ids_local = strategy_ids.reshape(rows)
    ids = jnp.concatenate([ids_local] + [swap(ids_local, "dp", k) for k in range(1, inner)])
    cot_own = jnp.concatenate(
        [features_of(cot_local, near)]
        + [swap(features_of(cot_local, near ^ k), "dp", k) for k in range(1, inner)]
    )
    weight = gather_line(out_weight, inner, outer, far)
    heads = gather_rows(head_out.reshape(rows, head_cols), inner)
    strategy_rows = jnp.concatenate(over_groups(features_of(strategy_table, near)), axis=1)
    cot = jnp.concatenate(over_groups(cot_own), axis=1)

    mixing = mixture(meta_graph)
    table = jnp.dot(mixing, strategy_rows.astype(jnp.float32), precision=highest)
    one_hot = (ids[:, None] == lax.broadcasted_iota(jnp.int32, (1, strategies), 1)).astype(
        jnp.float32
    )
    gating = 1.0 + jnp.dot(one_hot, table, precision=highest)
    grad_rows = (cot.astype(jnp.float32) * gating).astype(jnp.bfloat16)

    weight_part = lax.dot_general(
        grad_rows, heads, (((0,), (0,)), ((), ())), preferred_element_type=jnp.float32
    ).astype(jnp.bfloat16)
    weight_sum = scatter_line(weight_part, inner, outer, far)

    partial_sum = lax.dot_general(
        heads, weight, (((1,), (1,)), ((), ())), preferred_element_type=jnp.float32
    ).astype(jnp.bfloat16)
    head_part = jnp.dot(grad_rows, weight, preferred_element_type=jnp.float32).astype(jnp.bfloat16)
    head_grad = scatter_rows(head_part, inner).astype(jnp.bfloat16)

    def group_features(array, which):
        return lax.dynamic_slice_in_dim(array, which * width, width, 1)

    projected = group_features(partial_sum, group).astype(jnp.float32)
    for k in range(1, groups):
        projected = projected + swap(group_features(partial_sum, group ^ k), "mp", k).astype(
            jnp.float32
        )
    gated = (projected * group_features(gating, group)).astype(jnp.bfloat16)
    pieces = by_index(
        [gated[:rows]]
        + [swap(gated[k * rows:(k + 1) * rows], "dp", k) for k in range(1, inner)],
        near,
    )

    def spread(blocks):
        return jnp.concatenate(
            [p[:, s * block:(s + 1) * block] for s in range(spans) for p in blocks], axis=1
        )

    layer_out = (
        residual.reshape(rows, -1).astype(jnp.float32) + spread(pieces).astype(jnp.float32)
    ).astype(jnp.bfloat16)

    table_part = lax.dot_general(
        one_hot,
        cot_own.astype(jnp.float32) * projected,
        (((0,), (0,)), ((), ())),
        precision=highest,
        preferred_element_type=jnp.float32,
    )
    others = [swap(table_part, "dp", k * inner) for k in range(1, outer)]
    terms = by_index([table_part] + others, far)
    table_sum = terms[0]
    for term in terms[1:]:
        table_sum = table_sum + term
    table_grad = jnp.dot(mixing.T, table_sum, precision=highest) * grad_scale
    table_grad = spread(
        by_index([table_grad] + [swap(table_grad, "dp", k) for k in range(1, inner)], near)
    )
    return (
        layer_out.reshape(head_out.shape[:2] + (-1,)),
        head_grad.reshape(head_out.shape),
        weight_sum * grad_scale,
        table_grad,
    )


def solution(mesh):
    placed = (
        P(None, "dp", "mp"),
        P(None, "dp", "mp"),
        P("dp", "mp"),
        P(None, "mp"),
        P(),
        P(None, "dp"),
        P(None, "dp", "mp"),
    )
    return jax.shard_map(
        on_device,
        mesh=mesh,
        in_specs=placed,
        out_specs=(P(None, "dp", "mp"), P(None, "dp", "mp"), P("dp", "mp"), P(None, "mp")),
        check_vma=False,
    )
```

```python
import math

import jax
import jax.numpy as jnp
from jax import lax
from jax.sharding import PartitionSpec as P


def inner_size(count):
    return 1 << ((count.bit_length() - 1) // 2)


def mixture(meta_graph):
    counts = meta_graph.astype(jnp.float32)
    totals = jnp.maximum(jnp.sum(counts, axis=1, keepdims=True), 1.0)
    return jnp.eye(meta_graph.shape[0], dtype=jnp.float32) + counts / totals


def swap(value, axis, offset):
    count = lax.axis_size(axis)
    return lax.ppermute(value, axis, [(i, i ^ offset) for i in range(count)])


def by_index(relative, index):
    stacked = jnp.stack(relative)
    return [
        lax.dynamic_index_in_dim(stacked, index ^ place, 0, keepdims=False)
        for place in range(len(relative))
    ]


def bit_orders(inner):
    bits = [1 << b for b in range(inner.bit_length() - 1)]
    return bits, bits[::-1]


def key_order(bits):
    keys = [0]
    for bit in bits:
        keys = keys + [k ^ bit for k in keys]
    return keys


def after(value, *others):
    return lax.optimization_barrier((value,) + others)[0]


def line_pairs(inner, outer, step, first, last):
    return [
        (o * inner + i, (o + step) * inner + i) for o in range(first, last) for i in range(inner)
    ]


def gather_line(block, inner, outer, place):
    up, down, from_below, from_above = block, block, [], []
    for step in range(1, outer):
        up = lax.ppermute(up, "dp", line_pairs(inner, outer, 1, step - 1, outer - 1))
        down = lax.ppermute(down, "dp", line_pairs(inner, outer, -1, 1, outer - step + 1))
        from_below.append(up)
        from_above.append(down)
    return from_below, from_above


def join_line(block, from_below, from_above, outer, place):
    size = block.shape[0]
    whole = jnp.zeros((outer * size,) + block.shape[1:], block.dtype)
    whole = lax.dynamic_update_slice_in_dim(whole, block, place * size, 0)
    for step in range(1, outer):
        piece = jnp.where(place >= step, from_below[step - 1], from_above[outer - step - 1])
        spot = lax.rem(place - step + outer, outer) * size
        whole = lax.dynamic_update_slice_in_dim(whole, piece, spot, 0)
    return whole


def on_device(head_out, residual, out_weight, strategy_table, meta_graph, strategy_ids, cotangent):
    highest = lax.Precision.HIGHEST
    devices, groups = lax.axis_size("dp"), lax.axis_size("mp")
    inner = inner_size(devices)
    outer = devices // inner
    spans = outer // groups
    me, group = lax.axis_index("dp"), lax.axis_index("mp")
    near, far = lax.rem(me, inner), lax.div(me, inner)
    batches, local_rows, head_cols = head_out.shape
    rows = batches * local_rows
    strategies = meta_graph.shape[0]
    block = out_weight.shape[0]
    width = spans * block
    grad_scale = 1.0 / math.sqrt(batches * local_rows * devices)

    def features_of(array, which):
        return jnp.concatenate(
            [
                lax.dynamic_slice_in_dim(array, (s * inner + which) * block, block, 1)
                for s in range(spans)
            ],
            axis=1,
        )

    def over_groups(value):
        return by_index([value] + [swap(value, "mp", k) for k in range(1, groups)], group)

    cot_local = cotangent.reshape(rows, -1)
    ids_local = strategy_ids.reshape(rows)
    half = rows // 2
    orders = bit_orders(inner)
    keys = [key_order(bits) for bits in orders]

    def in_order(pieces):
        return jnp.concatenate(
            [pieces[k][s * half:(s + 1) * half] for s in range(2) for k in keys[s]]
        )

    ids = in_order([ids_local] + [swap(ids_local, "dp", k) for k in range(1, inner)])
    cot_own = in_order(
        [features_of(cot_local, near)]
        + [swap(features_of(cot_local, near ^ k), "dp", k) for k in range(1, inner)]
    )
    from_below, from_above = gather_line(out_weight, inner, outer, far)
    heads_local = head_out.reshape(rows, head_cols)
    sides = [heads_local[:half], heads_local[half:]]
    for step in range(len(orders[0])):
        for side in range(2):
            send = sides[side]
            if step:
                send = after(send, from_below[step - 1], from_above[step - 1])
            got = swap(send, "dp", orders[side][step])
            sides[side] = jnp.concatenate([sides[side], got])
    heads = jnp.concatenate(sides)
    weight = join_line(out_weight, from_below, from_above, outer, far)
    strategy_rows = jnp.concatenate(over_groups(features_of(strategy_table, near)), axis=1)
    cot = jnp.concatenate(over_groups(cot_own), axis=1)

    mixing = mixture(meta_graph)
    table = jnp.dot(mixing, strategy_rows.astype(jnp.float32), precision=highest)
    one_hot = (ids[:, None] == lax.broadcasted_iota(jnp.int32, (1, strategies), 1)).astype(
        jnp.float32
    )
    gating = 1.0 + jnp.dot(one_hot, table, precision=highest)
    grad_rows = (cot.astype(jnp.float32) * gating).astype(jnp.bfloat16)

    def weight_block(offset, source, kind):
        spot = lax.rem(far + offset, outer) * block
        return lax.dot_general(
            lax.dynamic_slice_in_dim(source, spot, block, 1),
            heads,
            (((0,), (0,)), ((), ())),
            preferred_element_type=jnp.float32,
        ).astype(kind)

    def head_rows(side, first, last):
        start = side * half * inner
        return jnp.dot(
            grad_rows[start + first * half:start + last * half],
            weight,
            preferred_element_type=jnp.float32,
        ).astype(jnp.bfloat16)

    blocks = {offset: weight_block(offset, grad_rows, jnp.bfloat16) for offset in {1, outer - 1}}
    line_up = [lax.ppermute(blocks[outer - 1], "dp", line_pairs(inner, outer, 1, 0, 1))]
    line_down = [lax.ppermute(blocks[1], "dp", line_pairs(inner, outer, -1, outer - 1, outer))]
    going = [head_rows(side, inner // 2, inner) for side in range(2)]
    kept = [head_rows(side, 0, inner // 2) for side in range(2)]
    came = [swap(going[side], "dp", orders[side][-1]) for side in range(2)]

    partial_sum = lax.dot_general(
        heads, weight, (((1,), (1,)), ((), ())), preferred_element_type=jnp.float32
    ).astype(jnp.bfloat16)
    later = after(grad_rows, *going)
    for offset in range(2, outer - 1):
        blocks[offset] = weight_block(offset, later, jnp.bfloat16)

    def group_features(array, which):
        return lax.dynamic_slice_in_dim(array, which * width, width, 1)

    projected = group_features(partial_sum, group).astype(jnp.float32)
    for k in range(1, groups):
        projected = projected + swap(group_features(partial_sum, group ^ k), "mp", k).astype(
            jnp.float32
        )
    gated = (projected * group_features(gating, group)).astype(jnp.bfloat16)

    def rows_for(key):
        starts = [(s * inner + keys[s].index(key)) * half for s in range(2)]
        return jnp.concatenate([gated[start:start + half] for start in starts])

    pieces = by_index(
        [rows_for(0)] + [swap(rows_for(k), "dp", k) for k in range(1, inner)], near
    )

    def spread(blocks):
        return jnp.concatenate(
            [p[:, s * block:(s + 1) * block] for s in range(spans) for p in blocks], axis=1
        )

    layer_out = (
        residual.reshape(rows, -1).astype(jnp.float32) + spread(pieces).astype(jnp.float32)
    ).astype(jnp.bfloat16)

    table_part = lax.dot_general(
        one_hot,
        cot_own.astype(jnp.float32) * projected,
        (((0,), (0,)), ((), ())),
        precision=highest,
        preferred_element_type=jnp.float32,
    )
    def add(left, right):
        return (left.astype(jnp.float32) + right.astype(jnp.float32)).astype(jnp.bfloat16)

    for step in range(2, outer):
        up = add(line_up[-1], blocks[outer - step])
        down = add(line_down[-1], blocks[step])
        if step == outer - 1:
            up, down = after(up, gated, table_part), after(down, gated, table_part)
        line_up.append(lax.ppermute(up, "dp", line_pairs(inner, outer, 1, 0, step)))
        line_down.append(
            lax.ppermute(down, "dp", line_pairs(inner, outer, -1, outer - step, outer))
        )
    own_block = weight_block(0, later, jnp.float32)
    weight_sum = own_block + (
        line_up[-1].astype(jnp.float32) + line_down[-1].astype(jnp.float32)
    )

    sums = []
    for side in range(2):
        total = add(kept[side], came[side])
        for bit in orders[side][-2::-1]:
            middle = total.shape[0] // 2
            arrived = swap(total[middle:], "dp", bit)
            total = add(total[:middle], arrived)
        sums.append(total)
    head_grad = jnp.concatenate(sums)

    others = [swap(table_part, "dp", k * inner) for k in range(1, outer)]
    terms = by_index([table_part] + others, far)
    table_sum = terms[0]
    for term in terms[1:]:
        table_sum = table_sum + term
    table_grad = jnp.dot(mixing.T, table_sum, precision=highest) * grad_scale
    table_grad = spread(
        by_index([table_grad] + [swap(table_grad, "dp", k) for k in range(1, inner)], near)
    )
    return (
        layer_out.reshape(head_out.shape[:2] + (-1,)),
        head_grad.reshape(head_out.shape),
        weight_sum * grad_scale,
        table_grad,
    )


def solution(mesh):
    placed = (
        P(None, "dp", "mp"),
        P(None, "dp", "mp"),
        P("dp", "mp"),
        P(None, "mp"),
        P(),
        P(None, "dp"),
        P(None, "dp", "mp"),
    )
    return jax.shard_map(
        on_device,
        mesh=mesh,
        in_specs=placed,
        out_specs=(P(None, "dp", "mp"), P(None, "dp", "mp"), P("dp", "mp"), P(None, "mp")),
        check_vma=False,
    )
```
